256 devices in a mesh: blk: 64 (over z, x, y_hi), grp: 4 (over y_lo, core).
Axes of the slice: x: 4, y: 4 (y_hi: 2, y_lo: 2; y = y_hi * 2 + y_lo), z: 8, core: 2. Of those that a mesh axis runs over, the one named last changes fastest.
Arguments:
- query_rows: bfloat16 [32768, 128], P(('blk', 'grp')), may hold values from -36 to 36
- key_rows: bfloat16 [32768, 128], P(('blk', 'grp')), may hold values from -6 to 6
- value_rows: bfloat16 [32768, 128], P(('blk', 'grp')), may hold values from -6 to 6
- query_tangent: bfloat16 [32768, 128], P(('blk', 'grp')), may hold values from -6 to 6
- key_tangent: bfloat16 [32768, 128], P(('blk', 'grp')), may hold values from -6 to 6
- value_tangent: bfloat16 [32768, 128], P(('blk', 'grp')), may hold values from -6 to 6
Outputs:
- attended: float32 [32768, 128], P(('blk', 'grp'))
- tangent_out: float32 [32768, 128], P(('blk', 'grp'))
The draws below stay inside these ranges and needn't reach their ends.
All inputs are finite; a program needn't handle non-finite values.
Results may differ from the reference program's by a relative error of at most 0.02.
Values may be sent and summed in bfloat16 or wider, within the bound.
A program may use at most 128 MiB of HBM per device.

```python
import math
import jax
import jax.numpy as jnp
from jax import lax

HD = 128
TOK_DEV = 128
SEQ = 32768
N_GRP = 4


def draw_query_rows(key, part):
    noise_key = jax.random.fold_in(key, 1)
    scale_key = jax.random.fold_in(key, 2)
    noise_field = jax.random.truncated_normal(noise_key, -6.0, 6.0, (SEQ, HD), jnp.float32)
    row_scale = jnp.exp(jax.random.uniform(scale_key, (SEQ, 1), jnp.float32, 0.0, math.log(6.0)))
    result = noise_field * row_scale
    return result.astype(jnp.bfloat16)


def draw_key_rows(key, part):
    noise_key = jax.random.fold_in(key, 3)
    result = jax.random.truncated_normal(noise_key, -6.0, 6.0, (SEQ, HD), jnp.float32)
    return result.astype(jnp.bfloat16)


def level_of(rng, shape, split, least, high):
    gain = 1.0
    for axis_at, parts in split:
        steps = jax.random.uniform(jax.random.fold_in(jax.random.fold_in(rng, 6), axis_at), (parts,), jnp.float32, least / len(split), high / len(split))
        gain = gain * jnp.repeat(jnp.exp(steps), shape[axis_at] // parts).reshape((-1,) + (1,) * (len(shape) - 1 - axis_at))
    return gain


def centred(key, dims, deviation, reach, cuts=(), kind=jnp.bfloat16):
    values = jax.random.normal(key, dims, jnp.float32) * deviation
    if len(cuts) > 0:
        values = level_of(key, dims, cuts, -0.22, 0.18) * values
    return jnp.clip(values, min=-reach, max=reach).astype(kind)


def setup_inputs(seed: int = 0) -> dict:
    streams_of = jax.random.split(jax.random.key(seed), 7)
    return {
        "query_rows": draw_query_rows(jax.random.fold_in(streams_of[6], 71), 0),
        "key_rows": draw_key_rows(jax.random.fold_in(streams_of[6], 71), 0),
        "value_rows": centred(streams_of[2], (SEQ, HD), 1.0, 6.0, ((0, 256),)),
        "query_tangent": centred(streams_of[3], (SEQ, HD), 1.0, 6.0, ((0, 256),)),
        "key_tangent": centred(streams_of[4], (SEQ, HD), 1.0, 6.0, ((0, 256),)),
        "value_tangent": centred(streams_of[5], (SEQ, HD), 1.0, 6.0, ((0, 256),)),
    }


def reference(query_rows, key_rows, value_rows, query_tangent, key_tangent, value_tangent):
    score_scale = HD ** -0.5
    span_rows = TOK_DEV * N_GRP

    def one_panel(pieces):
        query_part, tangent_part = pieces
        scores = jnp.dot(query_part, key_rows.T, preferred_element_type=jnp.float32) * score_scale
        slopes = (jnp.dot(tangent_part, key_rows.T, preferred_element_type=jnp.float32)
                  + jnp.dot(query_part, key_tangent.T, preferred_element_type=jnp.float32)) * score_scale
        row_max = jnp.max(scores, axis=1, keepdims=True)
        probs = jnp.exp(scores - row_max)
        row_total = jnp.sum(probs, axis=1, keepdims=True)
        weighted = probs * slopes
        slope_total = jnp.sum(weighted, axis=1, keepdims=True)
        probs_low = probs.astype(jnp.bfloat16)
        weighted_low = weighted.astype(jnp.bfloat16)
        primal_sum = jnp.dot(probs_low, value_rows, preferred_element_type=jnp.float32)
        tangent_sum = (jnp.dot(probs_low, value_tangent, preferred_element_type=jnp.float32)
                       + jnp.dot(weighted_low, value_rows, preferred_element_type=jnp.float32))
        attended = primal_sum / row_total
        tangent_out = tangent_sum / row_total - (slope_total / row_total) * attended
        return attended, tangent_out

    shaped = (query_rows.reshape(SEQ // span_rows, span_rows, HD),
              query_tangent.reshape(SEQ // span_rows, span_rows, HD))
    attended, tangent_out = lax.map(one_panel, shaped)
    return attended.reshape(SEQ, HD), tangent_out.reshape(SEQ, HD)
```

```python
import jax
import jax.numpy as jnp
from jax import lax
from jax.experimental import pallas as pl
from jax.experimental.pallas import tpu as pltpu
from jax.sharding import PartitionSpec as P

HD = 128
TOK = 128
F32, BF16 = jnp.float32, jnp.bfloat16
SCALE = HD ** -0.5
LOG2E = 1.4426950408889634
MESH = pl.DeviceIdType.MESH
NT = (((1,), (1,)), ((), ()))

REL = [(0, 0), (1, 0), (3, 0), (0, 1), (0, 3), (2, 0), (0, 2), (1, 1),
       (1, 3), (3, 1), (3, 3), (2, 1), (2, 3), (1, 2), (3, 2), (2, 2)]
BACK = [REL.index(((4 - a) % 4, (4 - b) % 4)) for a, b in REL]
NQ = 16 * TOK
NK = 16 * TOK
TQ, TK = 1024, 512


def lane_sum(v):
    out = v[:, :128]
    for j in range(1, v.shape[1] // 128):
        out = out + v[:, j * 128:(j + 1) * 128]
    return out


def kernel(q_ref, k_ref, v_ref, qt_ref, kt_ref, vt_ref, att_ref, tan_ref,
           kb, qb, acc, mb, lb, wb, osend, orecv, ssend, srecv, mix,
           q_s, q_r, ring_s, ring_r, part_s, part_r, o_s, o_r, st_s, st_r):
    blk, grp = lax.axis_index("blk"), lax.axis_index("grp")
    z, x = blk // 8, lax.rem(blk // 2, 4)
    y, core = lax.rem(blk, 2) * 2 + grp // 2, lax.rem(grp, 2)

    def dev(dz=0, dx=0, dy=0, dc=0):
        zz, xx, yy = lax.rem(z + dz, 8), lax.rem(x + dx, 4), lax.rem(y + dy, 4)
        return ((zz * 4 + xx) * 2 + yy // 2, lax.rem(yy, 2) * 2 + lax.rem(core + dc, 2))

    right, left, partner = dev(dz=1), dev(dz=7), dev(dc=1)
    peers = [dev(dx=a, dy=b) for a, b in REL]

    kb[0:TOK, 0:128] = kt_ref[...]
    kb[0:TOK, 128:256] = k_ref[...]
    kb[0:TOK, 256:384] = v_ref[...]
    kb[0:TOK, 384:512] = vt_ref[...]
    qb[0:TOK, 0:128] = q_ref[...]
    qb[0:TOK, 128:256] = qt_ref[...]

    barrier = pltpu.get_barrier_semaphore()
    for d in [right, left, partner] + peers[1:]:
        pl.semaphore_signal(barrier, inc=1, device_id=d, device_id_type=MESH)
    pl.semaphore_wait(barrier, 18)

    def copy(src, dst, ss, rs, to):
        return pltpu.make_async_remote_copy(src_ref=src, dst_ref=dst, send_sem=ss, recv_sem=rs,
                                            device_id=to, device_id_type=MESH)

    def own_rows(d):
        return kb.at[pl.ds(d * 256, TOK), :]

    def other_rows(d):
        return kb.at[pl.ds(d * 256 + TOK, TOK), :]

    def ring(d):
        if d < 7:
            src = 0 if d < 3 else d - 2
            return copy(own_rows(src), own_rows(d), ring_s.at[d], ring_r.at[d], right if d % 2 else left)
        src, off, to = (5, 0, right) if d == 7 else (6, 64, left)
        return copy(kb.at[pl.ds(src * 256 + off, 64), :], kb.at[pl.ds(7 * 256 + off, 64), :],
                    ring_s.at[d], ring_r.at[d], to)

    def across(d):
        return copy(own_rows(d), other_rows(d), part_s.at[d], part_r.at[d], partner)

    def query(s):
        b = BACK[s]
        return copy(qb.at[pl.ds(0, TOK), :], qb.at[pl.ds(b * TOK, TOK), :], q_s.at[b], q_r.at[b], peers[s])

    def result(s):
        b = BACK[s]
        return (copy(osend.at[s], orecv.at[b], o_s.at[b], o_r.at[b], peers[s]),
                copy(ssend.at[s], srecv.at[b], st_s.at[b], st_r.at[b], peers[s]))

    ring(1).start()
    ring(2).start()
    across(0).start()
    for s in range(1, 16):
        query(s).start()

    mb[...] = jnp.full_like(mb, -1e30)
    lb[...] = jnp.zeros_like(lb)
    wb[...] = jnp.zeros_like(wb)
    acc[...] = jnp.zeros_like(acc)

    def arrive(d):
        ring(d).wait_recv()
        if d < 7:
            ring(d + 2).start()
            across(d).start()

    def events(b):
        if b == 0:
            arrive(1)
            arrive(2)
            across(0).wait_recv()
            across(1).wait_recv()
            for s in range(1, 8):
                query(BACK[s]).wait_recv()
        elif b == 1:
            for s in range(8, 16):
                query(BACK[s]).wait_recv()
        elif b == 2:
            arrive(3)
            arrive(4)
            across(2).wait_recv()
            across(3).wait_recv()
        elif b == 4:
            arrive(5)
            arrive(6)
            across(4).wait_recv()
            across(5).wait_recv()
        elif b == 6:
            arrive(7)
            arrive(8)
            across(7).start()
            across(6).wait_recv()
            across(7).wait_recv()

    def finish(pn):
        rows = slice(pn * TQ, (pn + 1) * TQ)
        total = jnp.sum(lb[rows, :], axis=1, keepdims=True)
        inv = 1.0 / total
        slope = jnp.sum(wb[rows, :], axis=1, keepdims=True) * inv * SCALE
        att = acc[rows, :128] * inv
        tan = (acc[rows, 128:256] + SCALE * acc[rows, 256:384]) * inv - slope * att
        lane = lax.broadcasted_iota(jnp.int32, (TQ, 128), 1)
        stat = jnp.where(lane == 0, mb[rows, :], jnp.where(lane == 1, total, slope))
        for i in range(TQ // TOK):
            s = pn * (TQ // TOK) + i
            part = slice(i * TOK, (i + 1) * TOK)
            o_to, s_to = (orecv, srecv) if s == 0 else (osend, ssend)
            o_to[s, :, :128] = att[part].astype(BF16)
            o_to[s, :, 128:] = tan[part].astype(BF16)
            s_to[s] = stat[part].T[:8, :]
            if s > 0:
                for c in result(s):
                    c.start()

    def step(b, carry):
        for i in (0, 1, 2, 4, 6):
            @pl.when(b == i)
            def _():
                events(i)

        kp = b // 2
        pn = jnp.where(kp == 3, 1 - lax.rem(b, 2), lax.rem(b, 2))
        rows = pl.ds(pl.multiple_of(pn * TQ, TQ), TQ)
        keys = pl.ds(pl.multiple_of(kp * TK, TK), TK)
        s = lax.dot_general(qb[rows, :128], kb[keys, 128:256], NT, preferred_element_type=F32)
        t = lax.dot_general(qb[rows, :], kb[keys, :256], NT, preferred_element_type=F32)
        m = mb[rows, :]
        new = jnp.maximum(m, jnp.max(s, axis=1, keepdims=True) * (SCALE * LOG2E))
        al = jnp.exp2(m - new)
        p = jnp.exp2(s * (SCALE * LOG2E) - new[:, :1])
        w = p * t
        mb[rows, :] = new
        lb[rows, :] = lb[rows, :] * al + lane_sum(p)
        wb[rows, :] = wb[rows, :] * al + lane_sum(w)
        pv = jnp.dot(p.astype(BF16), kb[keys, 256:512], preferred_element_type=F32)
        wv = jnp.dot(w.astype(BF16), kb[keys, 256:384], preferred_element_type=F32)
        acc[rows, :128] = acc[rows, :128] * al + pv[:, :128]
        acc[rows, 128:256] = acc[rows, 128:256] * al + pv[:, 128:]
        acc[rows, 256:384] = acc[rows, 256:384] * al + wv

        @pl.when(b == 6)
        def _():
            finish(1)

        @pl.when(b == 7)
        def _():
            finish(0)
        return carry

    lax.fori_loop(0, 8, step, 0)

    for s in range(1, 16):
        for c in result(BACK[s]):
            c.wait_recv()
    st = srecv[...]
    m, l, sl = st[:, 0, :], st[:, 1, :], st[:, 2, :]
    wgt = jnp.exp2(m - jnp.max(m, axis=0, keepdims=True)) * l
    wgt = wgt / jnp.sum(wgt, axis=0, keepdims=True)
    mean = jnp.sum(wgt * sl, axis=0, keepdims=True)
    mix[...] = jnp.zeros_like(mix)
    mix[0:16, :] = wgt
    mix[16:32, :] = wgt * (sl - mean)
    col = mix[...].T
    att = jnp.zeros((TOK, HD), F32)
    tan = jnp.zeros((TOK, HD), F32)
    for s in range(16):
        a = orecv[s, :, :128].astype(F32)
        t = orecv[s, :, 128:].astype(F32)
        att = att + col[:, s:s + 1] * a
        tan = tan + col[:, s:s + 1] * t + col[:, 16 + s:17 + s] * a
    att_ref[...] = att
    tan_ref[...] = tan

    for d in range(1, 9):
        ring(d).wait_send()
    for d in range(8):
        across(d).wait_send()
    for s in range(1, 16):
        query(s).wait_send()
        for c in result(s):
            c.wait_send()


def on_device(query_rows, key_rows, value_rows, query_tangent, key_tangent, value_tangent):
    dma = pltpu.SemaphoreType.DMA
    return pl.pallas_call(
        kernel,
        out_shape=(jax.ShapeDtypeStruct((TOK, HD), F32),) * 2,
        in_specs=[pl.BlockSpec(memory_space=pltpu.VMEM)] * 6,
        out_specs=(pl.BlockSpec(memory_space=pltpu.VMEM),) * 2,
        scratch_shapes=[
            pltpu.VMEM((NK, 512), BF16),
            pltpu.VMEM((NQ, 256), BF16),
            pltpu.VMEM((NQ, 384), F32),
            pltpu.VMEM((NQ, 128), F32),
            pltpu.VMEM((NQ, 128), F32),
            pltpu.VMEM((NQ, 128), F32),
            pltpu.VMEM((16, TOK, 256), BF16),
            pltpu.VMEM((16, TOK, 256), BF16),
            pltpu.VMEM((16, 8, TOK), F32),
            pltpu.VMEM((16, 8, TOK), F32),
            pltpu.VMEM((TOK, TOK), F32),
            dma((16,)), dma((16,)), dma((9,)), dma((9,)), dma((8,)), dma((8,)),
            dma((16,)), dma((16,)), dma((16,)), dma((16,)),
        ],
        compiler_params=pltpu.CompilerParams(
            collective_id=0, has_side_effects=True, vmem_limit_bytes=56 << 20),
    )(query_rows, key_rows, value_rows, query_tangent, key_tangent, value_tangent)


def solution(mesh):
    placed = P(("blk", "grp"), None)
    return jax.shard_map(
        on_device,
        mesh=mesh,
        in_specs=(placed,) * 6,
        out_specs=(placed, placed),
        check_vma=False,
    )
```

```python
import jax
import jax.numpy as jnp
from jax import lax
from jax.experimental import pallas as pl
from jax.experimental.pallas import tpu as pltpu
from jax.sharding import PartitionSpec as P

HD = 128
TOK = 128
HALF = 64
F32, BF16 = jnp.float32, jnp.bfloat16
SCALE = HD ** -0.5
LOG2E = 1.4426950408889634
MESH = pl.DeviceIdType.MESH
NT = (((1,), (1,)), ((), ()))
NQ = 16 * TOK
NK = 16 * TOK

ROWS = ({1: 512, 3: 768, 2: 1536}, {1: 1024, 3: 1280, 2: 1792})
SMALL = [(0, 0), (1, 0), (2, 0), (0, 1), (1, 1), (2, 1)]
LARGE = [(3, 0), (3, 1), (1, 1), (2, 1), (0, 1)]


def lane_sum(v):
    out = v[:, :128]
    for j in range(1, v.shape[1] // 128):
        out = out + v[:, j * 128:(j + 1) * 128]
    return out


def pick(i, table):
    out = table[0]
    for n, v in enumerate(table):
        if n > 0:
            out = jnp.where(i == n, v, out)
    return out


def kernel(q_ref, k_ref, v_ref, qt_ref, kt_ref, vt_ref, att_ref, tan_ref,
           kb, qb, acc, mb, lb, wb, part, stat, part1, stat1, sum1, sstat1, part2, stat2,
           ring_s, ring_r, side_s, side_r, q1_s, q1_r, q2_s, q2_r, o1_s, o1_r, t1_s, t1_r, o2_s, o2_r, t2_s, t2_r):
    blk, grp = lax.axis_index("blk"), lax.axis_index("grp")
    z, x = blk // 8, lax.rem(blk // 2, 4)
    y, core = lax.rem(blk, 2) * 2 + grp // 2, lax.rem(grp, 2)

    def dev(dz=0, dx=0, dy=0, dc=0):
        zz, xx, yy = lax.rem(z + dz, 8), lax.rem(x + dx, 4), lax.rem(y + dy, 4)
        return ((zz * 4 + xx) * 2 + yy // 2, lax.rem(yy, 2) * 2 + lax.rem(core + dc, 2))

    right, left, partner = dev(dz=1), dev(dz=7), dev(dc=1)
    xs, ys = {i: dev(dx=i) for i in (1, 2, 3)}, {i: dev(dy=i) for i in (1, 2, 3)}

    kb[0:TOK, 0:128] = kt_ref[...]
    kb[0:TOK, 128:256] = k_ref[...]
    kb[0:TOK, 256:384] = v_ref[...]
    kb[0:TOK, 384:512] = vt_ref[...]
    for h in (0, 1):
        qb[h * 256:h * 256 + HALF, 0:128] = q_ref[h * HALF:(h + 1) * HALF, :]
        qb[h * 256:h * 256 + HALF, 128:256] = qt_ref[h * HALF:(h + 1) * HALF, :]

    barrier = pltpu.get_barrier_semaphore()
    for d in [right, left, partner] + list(xs.values()) + list(ys.values()):
        pl.semaphore_signal(barrier, inc=1, device_id=d, device_id_type=MESH)
    pl.semaphore_wait(barrier, 9)

    def copy(src, dst, ss, rs, to):
        return pltpu.make_async_remote_copy(src_ref=src, dst_ref=dst, send_sem=ss, recv_sem=rs,
                                            device_id=to, device_id_type=MESH)

    def key_half(d, h, side=0):
        return kb.at[pl.ds(d * 256 + side * TOK + h * HALF, HALF), :]

    def ring(d, h):
        src = 0 if d < 3 else (d - 2 if d < 7 else 5 + h)
        to = (right, left)[h] if d == 7 else (right if d % 2 else left)
        return copy(key_half(src, h), key_half(d, h), ring_s.at[d, h], ring_r.at[d, h], to)

    def across(d, h):
        return copy(key_half(d, h), key_half(d, h, 1), side_s.at[d, h], side_r.at[d, h], partner)

    def query1(h, i):
        b = 4 - i
        return copy(qb.at[pl.ds(h * 256, HALF), :], qb.at[pl.ds(h * 256 + b * HALF, HALF), :],
                    q1_s.at[h, b], q1_r.at[h, b], (xs, ys)[h][i])

    def query2(h, i):
        b = 4 - i
        return copy(qb.at[pl.ds(h * 256, 256), :], qb.at[pl.ds(ROWS[h][b], 256), :],
                    q2_s.at[h, b], q2_r.at[h, b], (ys, xs)[h][i])

    def result1(h, i):
        b, c = 4 - i, ROWS[h][i] // 256
        to = (ys, xs)[h][i]
        return (copy(part.at[c], part1.at[h, b - 1], o1_s.at[h, b], o1_r.at[h, b], to),
                copy(stat.at[c], stat1.at[h, b - 1], t1_s.at[h, b], t1_r.at[h, b], to))

    def result2(h, i):
        b = 4 - i
        to = (xs, ys)[h][i]
        return (copy(sum1.at[h, pl.ds(i * HALF, HALF), :], part2.at[h, b - 1], o2_s.at[h, b], o2_r.at[h, b], to),
                copy(sstat1.at[h], stat2.at[h, b - 1], t2_s.at[h, b], t2_r.at[h, b], to))

    for h in (0, 1):
        ring(1, h).start()
        ring(2, h).start()
        if h == 0:
            for i in (1, 3, 2):
                query1(0, i).start()
                query1(1, i).start()
        across(0, h).start()

    mb[...] = jnp.full_like(mb, -1e30)
    lb[...] = jnp.zeros_like(lb)
    wb[...] = jnp.zeros_like(wb)
    acc[...] = jnp.zeros_like(acc)

    def arrive(d, h):
        ring(d, h).wait_recv()
        if d < 5:
            ring(d + 2, h).start()
        elif d == 5 + h:
            ring(7, h).start()
        across(d, h).start()

    def side(*slots):
        for d in slots:
            across(d, 0).wait_recv()
            across(d, 1).wait_recv()

    def small_events(b):
        if b == 0:
            arrive(1, 0)
            arrive(2, 0)
            for i in (1, 3, 2):
                query1(0, i).wait_recv()
                query1(1, i).wait_recv()
            for i in (1, 3, 2):
                query2(0, i).start()
                query2(1, i).start()
            arrive(1, 1)
            arrive(2, 1)
            side(0, 1)
        elif b == 1:
            arrive(3, 0)
            arrive(4, 0)
            query2(0, 1).wait_recv()
            query2(0, 3).wait_recv()
        elif b == 2:
            arrive(3, 1)
            arrive(4, 1)
            query2(1, 1).wait_recv()
            query2(1, 3).wait_recv()
        elif b == 3:
            arrive(5, 0)
            arrive(6, 0)
            side(2, 3)
        elif b == 4:
            arrive(6, 1)
            arrive(5, 1)

    def large_events(b):
        if b == 0:
            arrive(7, 0)
            arrive(7, 1)
            query2(0, 2).wait_recv()
            query2(1, 2).wait_recv()
        elif b == 1:
            side(4, 5, 6, 7)

    def finish(g):
        rows = slice(g * 512, (g + 1) * 512)
        total = jnp.sum(lb[rows, :], axis=1, keepdims=True)
        inv = 1.0 / total
        slope = jnp.sum(wb[rows, :], axis=1, keepdims=True) * inv * SCALE
        att = acc[rows, :128] * inv
        tan = (acc[rows, 128:256] + SCALE * acc[rows, 256:384]) * inv - slope * att
        lane = lax.broadcasted_iota(jnp.int32, (512, 128), 1)
        col = jnp.where(lane == 0, mb[rows, :], jnp.where(lane == 1, total, slope))
        for i in (0, 1):
            c, here = 2 * g + i, slice(i * 256, (i + 1) * 256)
            part[c, :, :128] = att[here].astype(BF16)
            part[c, :, 128:] = tan[here].astype(BF16)
            for j in (0, 1):
                stat[c, :, j * 128:(j + 1) * 128] = col[i * 256 + j * 128:i * 256 + (j + 1) * 128].T[:8, :]
        for h, i in {1: [(0, 1), (0, 3)], 2: [(1, 1), (1, 3)], 3: [(0, 2), (1, 2)], 0: []}[g]:
            for c in result1(h, i):
                c.start()

    def attend(rows, keys):
        s = lax.dot_general(qb[rows, :128], kb[keys, 128:256], NT, preferred_element_type=F32)
        t = lax.dot_general(qb[rows, :], kb[keys, :256], NT, preferred_element_type=F32)
        m = mb[rows, :]
        new = jnp.maximum(m, jnp.max(s, axis=1, keepdims=True) * (SCALE * LOG2E))
        al = jnp.exp2(m - new)
        p = jnp.exp2(s * (SCALE * LOG2E) - new[:, :1])
        w = p * t
        mb[rows, :] = new
        lb[rows, :] = lb[rows, :] * al + lane_sum(p)
        wb[rows, :] = wb[rows, :] * al + lane_sum(w)
        pv = jnp.dot(p.astype(BF16), kb[keys, 256:512], preferred_element_type=F32)
        wv = jnp.dot(w.astype(BF16), kb[keys, 256:384], preferred_element_type=F32)
        acc[rows, :128] = acc[rows, :128] * al + pv[:, :128]
        acc[rows, 128:256] = acc[rows, 128:256] * al + pv[:, 128:]
        acc[rows, 256:384] = acc[rows, 256:384] * al + wv

    def small(b, carry):
        for i in range(5):
            @pl.when(b == i)
            def _():
                small_events(i)
        g, k = pick(b, [e[0] for e in SMALL]), pick(b, [e[1] for e in SMALL])
        attend(pl.ds(pl.multiple_of(g * 512, 512), 512), pl.ds(pl.multiple_of(k * 512, 512), 512))
        return carry

    def large(b, carry):
        for i in range(2):
            @pl.when(b == i)
            def _():
                large_events(i)
        g, k = pick(b, [e[0] for e in LARGE]), pick(b, [e[1] for e in LARGE])
        attend(pl.ds(pl.multiple_of(g * 512, 512), 512), pl.ds(pl.multiple_of(k * 1024, 1024), 1024))
        for i in range(1, 5):
            @pl.when(b == i)
            def _():
                finish(LARGE[i][0])
        return carry

    lax.fori_loop(0, len(SMALL), small, 0)
    lax.fori_loop(0, len(LARGE), large, 0)

    for h in (0, 1):
        for i in (1, 3, 2):
            for c in result1(h, i):
                c.wait_recv()
        stats = [stat[h]] + [stat1[h, j] for j in range(3)]
        m, l, sl = ([s[r:r + 1, :] for s in stats] for r in range(3))
        top = jnp.maximum(jnp.maximum(m[0], m[1]), jnp.maximum(m[2], m[3]))
        wgt = [jnp.exp2(a - top) * b for a, b in zip(m, l)]
        total = wgt[0] + wgt[1] + wgt[2] + wgt[3]
        inv = 1.0 / total
        wgt = [a * inv for a in wgt]
        mean = wgt[0] * sl[0] + wgt[1] * sl[1] + wgt[2] * sl[2] + wgt[3] * sl[3]
        sstat1[h, 0:1, :] = top
        sstat1[h, 1:2, :] = total
        sstat1[h, 2:3, :] = mean
        sstat1[h, 3:8, :] = jnp.zeros((5, 256), F32)
        both = jnp.concatenate(wgt + [a * (b - mean) for a, b in zip(wgt, sl)], axis=0)
        for j in (0, 1):
            rows = slice(j * 128, (j + 1) * 128)
            col = both[:, rows].T
            att = jnp.zeros((128, HD), F32)
            tan = jnp.zeros((128, HD), F32)
            for n in range(4):
                src = part[h, rows, :] if n == 0 else part1[h, n - 1, rows, :]
                a, t = src[:, :128].astype(F32), src[:, 128:].astype(F32)
                att = att + col[:, n:n + 1] * a
                tan = tan + col[:, n:n + 1] * t + col[:, 4 + n:5 + n] * a
            sum1[h, rows, :128] = att.astype(BF16)
            sum1[h, rows, 128:] = tan.astype(BF16)
        for i in (1, 3, 2):
            for c in result2(h, i):
                c.start()

    for h in (0, 1):
        for i in (1, 3, 2):
            for c in result2(h, i):
                c.wait_recv()
        cols = [sstat1[h, :, 0:128].T[0:HALF, :]]
        srcs = [sum1[h, 0:HALF, :]]
        for b in (1, 2, 3):
            at = (4 - b) * HALF
            lo = at // 128 * 128
            cols.append(stat2[h, b - 1, :, lo:lo + 128].T[at - lo:at - lo + HALF, :])
            srcs.append(part2[h, b - 1])
        m, l, sl = ([c[:, r:r + 1] for c in cols] for r in range(3))
        top = jnp.maximum(jnp.maximum(m[0], m[1]), jnp.maximum(m[2], m[3]))
        wgt = [jnp.exp2(a - top) * b for a, b in zip(m, l)]
        inv = 1.0 / (wgt[0] + wgt[1] + wgt[2] + wgt[3])
        wgt = [a * inv for a in wgt]
        mean = wgt[0] * sl[0] + wgt[1] * sl[1] + wgt[2] * sl[2] + wgt[3] * sl[3]
        att = jnp.zeros((HALF, HD), F32)
        tan = jnp.zeros((HALF, HD), F32)
        for n in range(4):
            a, t = srcs[n][:, :128].astype(F32), srcs[n][:, 128:].astype(F32)
            att = att + wgt[n] * a
            tan = tan + wgt[n] * t + (wgt[n] * (sl[n] - mean)) * a
        att_ref[h * HALF:(h + 1) * HALF, :] = att
        tan_ref[h * HALF:(h + 1) * HALF, :] = tan

    for h in (0, 1):
        for d in range(1, 8):
            ring(d, h).wait_send()
        for d in range(8):
            across(d, h).wait_send()
        for i in (1, 2, 3):
            query1(h, i).wait_send()
            query2(h, i).wait_send()
            for c in result1(h, i) + result2(h, i):
                c.wait_send()


def on_device(query_rows, key_rows, value_rows, query_tangent, key_tangent, value_tangent):
    dma = pltpu.SemaphoreType.DMA
    return pl.pallas_call(
        kernel,
        out_shape=(jax.ShapeDtypeStruct((TOK, HD), F32),) * 2,
        in_specs=[pl.BlockSpec(memory_space=pltpu.VMEM)] * 6,
        out_specs=(pl.BlockSpec(memory_space=pltpu.VMEM),) * 2,
        scratch_shapes=[
            pltpu.VMEM((NK, 512), BF16),
            pltpu.VMEM((NQ, 256), BF16),
            pltpu.VMEM((NQ, 384), F32),
            pltpu.VMEM((NQ, 128), F32),
            pltpu.VMEM((NQ, 128), F32),
            pltpu.VMEM((NQ, 128), F32),
            pltpu.VMEM((8, 256, 256), BF16),
            pltpu.VMEM((8, 8, 256), F32),
            pltpu.VMEM((2, 3, 256, 256), BF16),
            pltpu.VMEM((2, 3, 8, 256), F32),
            pltpu.VMEM((2, 256, 256), BF16),
            pltpu.VMEM((2, 8, 256), F32),
            pltpu.VMEM((2, 3, HALF, 256), BF16),
            pltpu.VMEM((2, 3, 8, 256), F32),
            dma((8, 2)), dma((8, 2)), dma((8, 2)), dma((8, 2)),
            dma((2, 4)), dma((2, 4)), dma((2, 4)), dma((2, 4)),
            dma((2, 4)), dma((2, 4)), dma((2, 4)), dma((2, 4)),
            dma((2, 4)), dma((2, 4)), dma((2, 4)), dma((2, 4)),
        ],
        compiler_params=pltpu.CompilerParams(
            collective_id=0, has_side_effects=True, vmem_limit_bytes=56 << 20),
    )(query_rows, key_rows, value_rows, query_tangent, key_tangent, value_tangent)


def solution(mesh):
    placed = P(("blk", "grp"), None)
    return jax.shard_map(
        on_device,
        mesh=mesh,
        in_specs=(placed,) * 6,
        out_specs=(placed, placed),
        check_vma=False,
    )
```

```python
import jax
import jax.numpy as jnp
from jax import lax
from jax.experimental import pallas as pl
from jax.experimental.pallas import tpu as pltpu
from jax.sharding import PartitionSpec as P

HD = 128
TOK = 128
HALF = 64
F32, BF16 = jnp.float32, jnp.bfloat16
SCALE = HD ** -0.5
LOG2E = 1.4426950408889634
MESH = pl.DeviceIdType.MESH
NT = (((1,), (1,)), ((), ()))
NQ = 16 * TOK
NK = 16 * TOK

UNIT = ({1: (4, 8), 3: (5, 9), 2: (12, 13)}, {1: (6, 10), 3: (7, 11), 2: (14, 15)})
SENT = {UNIT[h][i][p]: (h, i, p) for h in (0, 1) for i in (1, 2, 3) for p in (0, 1)}
SMALL = [(0, 0), (1, 0), (2, 0), (0, 1), (1, 1), (2, 1)]
LARGE = [(3, 0), (3, 1), (1, 1), (2, 1), (0, 1)]


def pick(i, table):
    out = table[0]
    for n, v in enumerate(table):
        if n > 0:
            out = jnp.where(i == n, v, out)
    return out


def kernel(q_ref, k_ref, v_ref, qt_ref, kt_ref, vt_ref, att_ref, tan_ref,
           kb, qb, acc, mb, lb, wb, part, stat, part1, stat1, sum1, sstat1, part2, stat2,
           in_s, ring_s, ring_r, side_s, side_r, q1_s, q1_r, q2_s, q2_r, o1_s, o1_r, t1_s, t1_r, o2_s, o2_r, t2_s, t2_r):
    blk, grp = lax.axis_index("blk"), lax.axis_index("grp")
    z, x = blk // 8, lax.rem(blk // 2, 4)
    y, core = lax.rem(blk, 2) * 2 + grp // 2, lax.rem(grp, 2)

    def dev(dz=0, dx=0, dy=0, dc=0):
        zz, xx, yy = lax.rem(z + dz, 8), lax.rem(x + dx, 4), lax.rem(y + dy, 4)
        return ((zz * 4 + xx) * 2 + yy // 2, lax.rem(yy, 2) * 2 + lax.rem(core + dc, 2))

    right, left, partner = dev(dz=1), dev(dz=7), dev(dc=1)
    xs, ys = {i: dev(dx=i) for i in (1, 2, 3)}, {i: dev(dy=i) for i in (1, 2, 3)}

    barrier = pltpu.get_barrier_semaphore()
    for d in [right, left, partner] + list(xs.values()) + list(ys.values()):
        pl.semaphore_signal(barrier, inc=1, device_id=d, device_id_type=MESH)

    loads = [pltpu.make_async_copy(src, kb.at[pl.ds(0, TOK), pl.ds(n * HD, HD)], in_s.at[n])
             for n, src in enumerate((kt_ref, k_ref, v_ref, vt_ref))]
    for h in (0, 1):
        for n, src in enumerate((q_ref, qt_ref)):
            loads.append(pltpu.make_async_copy(src.at[pl.ds(h * HALF, HALF), :],
                                               qb.at[pl.ds(h * 256, HALF), pl.ds(n * HD, HD)], in_s.at[4 + 2 * h + n]))
    for c in loads:
        c.start()
    for c in loads:
        c.wait()
    pl.semaphore_wait(barrier, 9)

    def copy(src, dst, ss, rs, to):
        return pltpu.make_async_remote_copy(src_ref=src, dst_ref=dst, send_sem=ss, recv_sem=rs,
                                            device_id=to, device_id_type=MESH)

    def key_half(d, h, side=0):
        return kb.at[pl.ds(d * 256 + side * TOK + h * HALF, HALF), :]

    def ring(d, h):
        src = 0 if d < 3 else (d - 2 if d < 7 else 5 + h)
        to = (right, left)[h] if d == 7 else (right if d % 2 else left)
        return copy(key_half(src, h), key_half(d, h), ring_s.at[d, h], ring_r.at[d, h], to)

    def across(d, h):
        return copy(key_half(d, h), key_half(d, h, 1), side_s.at[d, h], side_r.at[d, h], partner)

    def query1(h, i):
        b = 4 - i
        return copy(qb.at[pl.ds(h * 256, HALF), :], qb.at[pl.ds(h * 256 + b * HALF, HALF), :],
                    q1_s.at[h, b], q1_r.at[h, b], (xs, ys)[h][i])

    def query2(h, i, p):
        b = 4 - i
        return copy(qb.at[pl.ds(h * 256 + p * TOK, TOK), :], qb.at[pl.ds(UNIT[h][b][p] * TOK, TOK), :],
                    q2_s.at[h, 2 * b + p], q2_r.at[h, 2 * b + p], (ys, xs)[h][i])

    def result1(h, i, p):
        b, u = 4 - i, UNIT[h][i][p]
        to, n = (ys, xs)[h][i], 2 * b + p
        return (copy(part.at[u], part1.at[h, b - 1, p], o1_s.at[h, n], o1_r.at[h, n], to),
                copy(stat.at[u], stat1.at[h, b - 1, p], t1_s.at[h, n], t1_r.at[h, n], to))

    def result2(h, i):
        b, p = 4 - i, i // 2
        to = (xs, ys)[h][i]
        return (copy(sum1.at[h, p, pl.ds(i % 2 * HALF, HALF), :], part2.at[h, b - 1], o2_s.at[h, b], o2_r.at[h, b], to),
                copy(sstat1.at[h, p], stat2.at[h, b - 1], t2_s.at[h, b], t2_r.at[h, b], to))

    for h in (0, 1):
        ring(1, h).start()
        ring(2, h).start()
        if h == 0:
            for i in (1, 3, 2):
                query1(0, i).start()
                query1(1, i).start()
        across(0, h).start()

    mb[...] = jnp.full_like(mb, -1e30)
    lb[...] = jnp.zeros_like(lb)
    wb[...] = jnp.zeros_like(wb)
    acc[...] = jnp.zeros_like(acc)

    def arrive(d, h):
        ring(d, h).wait_recv()
        if d < 5:
            ring(d + 2, h).start()
        elif d == 5 + h:
            ring(7, h).start()
        across(d, h).start()

    def side(*slots):
        for d in slots:
            across(d, 0).wait_recv()
            across(d, 1).wait_recv()

    def small_events(b):
        if b == 0:
            arrive(1, 0)
            arrive(2, 0)
            for i in (1, 3, 2):
                query1(0, i).wait_recv()
                query1(1, i).wait_recv()
            for p, i in ((0, 1), (0, 3), (1, 1), (1, 3), (0, 2), (1, 2)):
                query2(0, i, p).start()
                query2(1, i, p).start()
            arrive(1, 1)
            arrive(2, 1)
            side(0, 1)
        elif b == 1:
            arrive(3, 0)
            arrive(4, 0)
            near(0)
        elif b == 2:
            arrive(3, 1)
            arrive(4, 1)
            near(1)
        elif b == 3:
            side(2, 3)
        elif b == 4:
            arrive(5, 0)
            arrive(6, 0)
        elif b == 5:
            arrive(6, 1)
            arrive(5, 1)

    def near(p):
        for i in (1, 3):
            query2(0, i, p).wait_recv()
            query2(1, i, p).wait_recv()

    def large_events(b):
        if b == 0:
            for p in (0, 1):
                query2(0, 2, p).wait_recv()
                query2(1, 2, p).wait_recv()
            arrive(7, 0)
            arrive(7, 1)
        elif b == 1:
            side(4, 5, 6, 7)

    def finish(g):
        for u in range(4 * g, 4 * g + 4):
            rows = slice(u * TOK, (u + 1) * TOK)
            total = jnp.sum(lb[rows, :], axis=1, keepdims=True)
            inv = 1.0 / total
            slope = jnp.sum(wb[rows, :], axis=1, keepdims=True) * inv * SCALE
            att = acc[rows, :128] * inv
            tan = (acc[rows, 128:256] + SCALE * acc[rows, 256:384]) * inv - slope * att
            part[u, :, :128] = att.astype(BF16)
            part[u, :, 128:] = tan.astype(BF16)
            lane = lax.broadcasted_iota(jnp.int32, (TOK, 128), 1)
            stat[u] = jnp.where(lane == 0, mb[rows, :], jnp.where(lane == 1, total, slope)).T[:8, :]
            if u >= 4:
                for c in result1(*SENT[u]):
                    c.start()

    def attend(rows, keys, groups):
        s = lax.dot_general(qb[rows, :128], kb[keys, 128:256], NT, preferred_element_type=F32)
        t = lax.dot_general(qb[rows, :], kb[keys, :256], NT, preferred_element_type=F32)
        cut = [slice(j * 128, (j + 1) * 128) for j in range(groups)]
        top = s[:, cut[0]]
        for j in cut[1:]:
            top = jnp.maximum(top, s[:, j])
        top = jnp.broadcast_to(jnp.max(top, axis=1, keepdims=True), top.shape) * (SCALE * LOG2E)
        m = mb[rows, :]
        new = jnp.maximum(m, top)
        al = jnp.exp2(m - new)
        p = [jnp.exp2(s[:, j] * (SCALE * LOG2E) - new) for j in cut]
        w = [a * t[:, j] for a, j in zip(p, cut)]
        mb[rows, :] = new
        lb[rows, :] = lb[rows, :] * al + sum(p[1:], p[0])
        wb[rows, :] = wb[rows, :] * al + sum(w[1:], w[0])
        p = jnp.concatenate([a.astype(BF16) for a in p], axis=1)
        w = jnp.concatenate([a.astype(BF16) for a in w], axis=1)
        pv = jnp.dot(p, kb[keys, 256:512], preferred_element_type=F32)
        wv = jnp.dot(w, kb[keys, 256:384], preferred_element_type=F32)
        acc[rows, :128] = acc[rows, :128] * al + pv[:, :128]
        acc[rows, 128:256] = acc[rows, 128:256] * al + pv[:, 128:]
        acc[rows, 256:384] = acc[rows, 256:384] * al + wv

    def small(b, carry):
        for i in range(6):
            @pl.when(b == i)
            def _():
                small_events(i)
        g, k = pick(b, [e[0] for e in SMALL]), pick(b, [e[1] for e in SMALL])
        attend(pl.ds(pl.multiple_of(g * 512, 512), 512), pl.ds(pl.multiple_of(k * 512, 512), 512), 4)
        return carry

    def large(b, carry):
        for i in range(2):
            @pl.when(b == i)
            def _():
                large_events(i)
        g, k = pick(b, [e[0] for e in LARGE]), pick(b, [e[1] for e in LARGE])
        attend(pl.ds(pl.multiple_of(g * 512, 512), 512), pl.ds(pl.multiple_of(k * 1024, 1024), 1024), 8)
        for i in range(1, 5):
            @pl.when(b == i)
            def _():
                finish(LARGE[i][0])
        return carry

    lax.fori_loop(0, len(SMALL), small, 0)
    lax.fori_loop(0, len(LARGE), large, 0)

    for p, h in ((0, 0), (0, 1), (1, 0), (1, 1)):
        for i in (2, 1, 3):
            for c in result1(h, i, p):
                c.wait_recv()
        stats = [stat[2 * h + p]] + [stat1[h, j, p] for j in range(3)]
        m, l, sl = ([s[r:r + 1, :] for s in stats] for r in range(3))
        top = jnp.maximum(jnp.maximum(m[0], m[1]), jnp.maximum(m[2], m[3]))
        wgt = [jnp.exp2(a - top) * b for a, b in zip(m, l)]
        total = wgt[0] + wgt[1] + wgt[2] + wgt[3]
        inv = 1.0 / total
        wgt = [a * inv for a in wgt]
        mean = wgt[0] * sl[0] + wgt[1] * sl[1] + wgt[2] * sl[2] + wgt[3] * sl[3]
        sstat1[h, p, 0:1, :] = top
        sstat1[h, p, 1:2, :] = total
        sstat1[h, p, 2:3, :] = mean
        sstat1[h, p, 3:8, :] = jnp.zeros((5, TOK), F32)
        col = jnp.concatenate(wgt + [a * (b - mean) for a, b in zip(wgt, sl)], axis=0).T
        att = jnp.zeros((TOK, HD), F32)
        tan = jnp.zeros((TOK, HD), F32)
        for n in range(4):
            src = part[2 * h + p] if n == 0 else part1[h, n - 1, p]
            a, t = src[:, :128].astype(F32), src[:, 128:].astype(F32)
            att = att + col[:, n:n + 1] * a
            tan = tan + col[:, n:n + 1] * t + col[:, 4 + n:5 + n] * a
        sum1[h, p, :, :128] = att.astype(BF16)
        sum1[h, p, :, 128:] = tan.astype(BF16)
        for i in ((1,), (2, 3))[p]:
            for c in result2(h, i):
                c.start()

    for h in (0, 1):
        for i in (1, 3, 2):
            for c in result2(h, i):
                c.wait_recv()
        cols = [sstat1[h, 0].T[0:HALF, :]]
        srcs = [sum1[h, 0, 0:HALF, :]]
        for b in (1, 2, 3):
            at = (4 - b) % 2 * HALF
            cols.append(stat2[h, b - 1].T[at:at + HALF, :])
            srcs.append(part2[h, b - 1])
        m, l, sl = ([c[:, r:r + 1] for c in cols] for r in range(3))
        top = jnp.maximum(jnp.maximum(m[0], m[1]), jnp.maximum(m[2], m[3]))
        wgt = [jnp.exp2(a - top) * b for a, b in zip(m, l)]
        inv = 1.0 / (wgt[0] + wgt[1] + wgt[2] + wgt[3])
        wgt = [a * inv for a in wgt]
        mean = wgt[0] * sl[0] + wgt[1] * sl[1] + wgt[2] * sl[2] + wgt[3] * sl[3]
        att = jnp.zeros((HALF, HD), F32)
        tan = jnp.zeros((HALF, HD), F32)
        for n in range(4):
            a, t = srcs[n][:, :128].astype(F32), srcs[n][:, 128:].astype(F32)
            att = att + wgt[n] * a
            tan = tan + wgt[n] * t + (wgt[n] * (sl[n] - mean)) * a
        att_ref[h * HALF:(h + 1) * HALF, :] = att
        tan_ref[h * HALF:(h + 1) * HALF, :] = tan

    for h in (0, 1):
        for d in range(1, 8):
            ring(d, h).wait_send()
        for d in range(8):
            across(d, h).wait_send()
        for i in (1, 2, 3):
            query1(h, i).wait_send()
            query2(h, i, 0).wait_send()
            query2(h, i, 1).wait_send()
            for c in result1(h, i, 0) + result1(h, i, 1) + result2(h, i):
                c.wait_send()


def on_device(query_rows, key_rows, value_rows, query_tangent, key_tangent, value_tangent):
    dma = pltpu.SemaphoreType.DMA
    return pl.pallas_call(
        kernel,
        out_shape=(jax.ShapeDtypeStruct((TOK, HD), F32),) * 2,
        in_specs=[pl.BlockSpec(memory_space=pl.ANY)] * 6,
        out_specs=(pl.BlockSpec(memory_space=pltpu.VMEM),) * 2,
        scratch_shapes=[
            pltpu.VMEM((NK, 512), BF16),
            pltpu.VMEM((NQ, 256), BF16),
            pltpu.VMEM((NQ, 384), F32),
            pltpu.VMEM((NQ, 128), F32),
            pltpu.VMEM((NQ, 128), F32),
            pltpu.VMEM((NQ, 128), F32),
            pltpu.VMEM((16, TOK, 256), BF16),
            pltpu.VMEM((16, 8, TOK), F32),
            pltpu.VMEM((2, 3, 2, TOK, 256), BF16),
            pltpu.VMEM((2, 3, 2, 8, TOK), F32),
            pltpu.VMEM((2, 2, TOK, 256), BF16),
            pltpu.VMEM((2, 2, 8, TOK), F32),
            pltpu.VMEM((2, 3, HALF, 256), BF16),
            pltpu.VMEM((2, 3, 8, TOK), F32),
            dma((8,)), dma((8, 2)), dma((8, 2)), dma((8, 2)), dma((8, 2)),
            dma((2, 4)), dma((2, 4)), dma((2, 8)), dma((2, 8)),
            dma((2, 8)), dma((2, 8)), dma((2, 8)), dma((2, 8)),
            dma((2, 4)), dma((2, 4)), dma((2, 4)), dma((2, 4)),
        ],
        compiler_params=pltpu.CompilerParams(
            collective_id=0, has_side_effects=True, vmem_limit_bytes=56 << 20),
    )(query_rows, key_rows, value_rows, query_tangent, key_tangent, value_tangent)


def solution(mesh):
    placed = P(("blk", "grp"), None)
    return jax.shard_map(
        on_device,
        mesh=mesh,
        in_specs=(placed,) * 6,
        out_specs=(placed, placed),
        check_vma=False,
    )
```

```python
import jax
import jax.numpy as jnp
from jax import lax
from jax.experimental import pallas as pl
from jax.experimental.pallas import tpu as pltpu
from jax.sharding import PartitionSpec as P

HD = 128
TOK = 128
HALF = 64
F32, BF16 = jnp.float32, jnp.bfloat16
SCALE = HD ** -0.5
LOG2E = 1.4426950408889634
MESH = pl.DeviceIdType.MESH
NT = (((1,), (1,)), ((), ()))
NQ = 16 * TOK
NK = 16 * TOK

UNIT = ({1: (4, 8), 3: (5, 9), 2: (12, 13)}, {1: (6, 10), 3: (7, 11), 2: (14, 15)})
SENT = {UNIT[h][i][p]: (h, i, p) for h in (0, 1) for i in (1, 2, 3) for p in (0, 1)}
SMALL = [(0, 0), (1, 0), (2, 0), (0, 1), (1, 1), (2, 1)]
LARGE = [(3, 0), (3, 1), (1, 1), (2, 1), (0, 1)]


def pick(i, table):
    out = table[0]
    for n, v in enumerate(table):
        if n > 0:
            out = jnp.where(i == n, v, out)
    return out


def kernel(q_ref, k_ref, v_ref, qt_ref, kt_ref, vt_ref, out_ref,
           kb, qb, acc, mb, lb, wb, part, stat, part1, stat1, sum1, sstat1, part2, stat2,
           in_s, ring_s, ring_r, side_s, side_r, q1_s, q1_r, q2_s, q2_r, o1_s, o1_r, t1_s, t1_r, o2_s, o2_r, t2_s, t2_r):
    blk, grp = lax.axis_index("blk"), lax.axis_index("grp")
    z, x = blk // 8, lax.rem(blk // 2, 4)
    y, core = lax.rem(blk, 2) * 2 + grp // 2, lax.rem(grp, 2)

    def dev(dz=0, dx=0, dy=0, dc=0):
        zz, xx, yy = lax.rem(z + dz, 8), lax.rem(x + dx, 4), lax.rem(y + dy, 4)
        return ((zz * 4 + xx) * 2 + yy // 2, lax.rem(yy, 2) * 2 + lax.rem(core + dc, 2))

    right, left, partner = dev(dz=1), dev(dz=7), dev(dc=1)
    xs, ys = {i: dev(dx=i) for i in (1, 2, 3)}, {i: dev(dy=i) for i in (1, 2, 3)}

    barrier = pltpu.get_barrier_semaphore()
    for d in [right, left, partner] + list(xs.values()) + list(ys.values()):
        pl.semaphore_signal(barrier, inc=1, device_id=d, device_id_type=MESH)

    loads = [pltpu.make_async_copy(src, kb.at[pl.ds(0, TOK), pl.ds(n * HD, HD)], in_s.at[n])
             for n, src in enumerate((kt_ref, k_ref, v_ref, vt_ref))]
    for h in (0, 1):
        for n, src in enumerate((q_ref, qt_ref)):
            loads.append(pltpu.make_async_copy(src.at[pl.ds(h * HALF, HALF), :],
                                               qb.at[pl.ds(h * 256, HALF), pl.ds(n * HD, HD)], in_s.at[4 + 2 * h + n]))
    for c in loads:
        c.start()
    for c in loads:
        c.wait()
    pl.semaphore_wait(barrier, 9)

    def copy(src, dst, ss, rs, to):
        return pltpu.make_async_remote_copy(src_ref=src, dst_ref=dst, send_sem=ss, recv_sem=rs,
                                            device_id=to, device_id_type=MESH)

    def key_half(d, h, side=0):
        return kb.at[pl.ds(d * 256 + side * TOK + h * HALF, HALF), :]

    def ring(d, h):
        src = 0 if d < 3 else (d - 2 if d < 7 else 5 + h)
        to = (right, left)[h] if d == 7 else (right if d % 2 else left)
        return copy(key_half(src, h), key_half(d, h), ring_s.at[d, h], ring_r.at[d, h], to)

    def across(d, h):
        return copy(key_half(d, h), key_half(d, h, 1), side_s.at[d, h], side_r.at[d, h], partner)

    def query1(h, i):
        b = 4 - i
        return copy(qb.at[pl.ds(h * 256, HALF), :], qb.at[pl.ds(h * 256 + b * HALF, HALF), :],
                    q1_s.at[h, b], q1_r.at[h, b], (xs, ys)[h][i])

    def query2(h, i, p):
        b = 4 - i
        return copy(qb.at[pl.ds(h * 256 + p * TOK, TOK), :], qb.at[pl.ds(UNIT[h][b][p] * TOK, TOK), :],
                    q2_s.at[h, 2 * b + p], q2_r.at[h, 2 * b + p], (ys, xs)[h][i])

    def result1(h, i, p):
        b, u = 4 - i, UNIT[h][i][p]
        to, n = (ys, xs)[h][i], 2 * b + p
        return (copy(part.at[u], part1.at[h, b - 1, p], o1_s.at[h, n], o1_r.at[h, n], to),
                copy(stat.at[u], stat1.at[h, b - 1, p], t1_s.at[h, n], t1_r.at[h, n], to))

    def result2(h, i):
        b, p = 4 - i, i // 2
        to = (xs, ys)[h][i]
        return (copy(sum1.at[h, p, pl.ds(i % 2 * HALF, HALF), :], part2.at[h, b - 1], o2_s.at[h, b], o2_r.at[h, b], to),
                copy(sstat1.at[h, p], stat2.at[h, b - 1], t2_s.at[h, b], t2_r.at[h, b], to))

    for h in (0, 1):
        ring(1, h).start()
        ring(2, h).start()
        if h == 0:
            for i in (1, 3, 2):
                query1(0, i).start()
                query1(1, i).start()
        across(0, h).start()

    mb[...] = jnp.full_like(mb, -1e30)
    lb[...] = jnp.zeros_like(lb)
    wb[...] = jnp.zeros_like(wb)
    acc[...] = jnp.zeros_like(acc)

    def arrive(d, h):
        ring(d, h).wait_recv()
        if d < 5:
            ring(d + 2, h).start()
        elif d == 5 + h:
            ring(7, h).start()
        across(d, h).start()

    def side(*slots):
        for d in slots:
            across(d, 0).wait_recv()
            across(d, 1).wait_recv()

    def small_events(b):
        if b == 0:
            arrive(1, 0)
            arrive(2, 0)
            for i in (1, 3, 2):
                query1(0, i).wait_recv()
                query1(1, i).wait_recv()
            for p, i in ((0, 1), (0, 3), (1, 1), (1, 3), (0, 2), (1, 2)):
                query2(0, i, p).start()
                query2(1, i, p).start()
            arrive(1, 1)
            arrive(2, 1)
            side(0, 1)
        elif b == 1:
            arrive(3, 0)
            arrive(4, 0)
            near(0)
        elif b == 2:
            arrive(3, 1)
            arrive(4, 1)
            near(1)
        elif b == 3:
            side(2, 3)
        elif b == 4:
            arrive(5, 0)
            arrive(6, 0)
        elif b == 5:
            arrive(6, 1)
            arrive(5, 1)

    def near(p):
        for i in (1, 3):
            query2(0, i, p).wait_recv()
            query2(1, i, p).wait_recv()

    def large_events(b):
        if b == 0:
            for p in (0, 1):
                query2(0, 2, p).wait_recv()
                query2(1, 2, p).wait_recv()
            arrive(7, 0)
            arrive(7, 1)
        elif b == 1:
            side(4, 5, 6, 7)

    def finish(g):
        for u in range(4 * g, 4 * g + 4):
            rows = slice(u * TOK, (u + 1) * TOK)
            total = jnp.sum(lb[rows, :], axis=1, keepdims=True)
            inv = 1.0 / total
            slope = jnp.sum(wb[rows, :], axis=1, keepdims=True) * inv * SCALE
            att = acc[rows, :128] * inv
            tan = (acc[rows, 128:256] + SCALE * acc[rows, 256:384]) * inv - slope * att
            part[u, :, :128] = att.astype(BF16)
            part[u, :, 128:] = tan.astype(BF16)
            lane = lax.broadcasted_iota(jnp.int32, (TOK, 128), 1)
            stat[u] = jnp.where(lane == 0, mb[rows, :], jnp.where(lane == 1, total, slope)).T[:8, :]
            if u >= 4:
                for c in result1(*SENT[u]):
                    c.start()

    def attend(rows, keys, groups):
        s = lax.dot_general(qb[rows, :128], kb[keys, 128:256], NT, preferred_element_type=F32)
        t = lax.dot_general(qb[rows, :], kb[keys, :256], NT, preferred_element_type=F32)
        cut = [slice(j * 128, (j + 1) * 128) for j in range(groups)]
        top = s[:, cut[0]]
        for j in cut[1:]:
            top = jnp.maximum(top, s[:, j])
        top = jnp.broadcast_to(jnp.max(top, axis=1, keepdims=True), top.shape) * (SCALE * LOG2E)
        m = mb[rows, :]
        new = jnp.maximum(m, top)
        al = jnp.exp2(m - new)
        p = [jnp.exp2(s[:, j] * (SCALE * LOG2E) - new) for j in cut]
        w = [a * t[:, j] for a, j in zip(p, cut)]
        mb[rows, :] = new
        lb[rows, :] = lb[rows, :] * al + sum(p[1:], p[0])
        wb[rows, :] = wb[rows, :] * al + sum(w[1:], w[0])
        p = jnp.concatenate([a.astype(BF16) for a in p], axis=1)
        w = jnp.concatenate([a.astype(BF16) for a in w], axis=1)
        pv = jnp.dot(p, kb[keys, 256:512], preferred_element_type=F32)
        wv = jnp.dot(w, kb[keys, 256:384], preferred_element_type=F32)
        acc[rows, :128] = acc[rows, :128] * al + pv[:, :128]
        acc[rows, 128:256] = acc[rows, 128:256] * al + pv[:, 128:]
        acc[rows, 256:384] = acc[rows, 256:384] * al + wv

    def small(b, carry):
        for i in range(6):
            @pl.when(b == i)
            def _():
                small_events(i)
        g, k = pick(b, [e[0] for e in SMALL]), pick(b, [e[1] for e in SMALL])
        attend(pl.ds(pl.multiple_of(g * 512, 512), 512), pl.ds(pl.multiple_of(k * 512, 512), 512), 4)
        return carry

    def large(b, carry):
        for i in range(2):
            @pl.when(b == i)
            def _():
                large_events(i)
        g, k = pick(b, [e[0] for e in LARGE]), pick(b, [e[1] for e in LARGE])
        attend(pl.ds(pl.multiple_of(g * 512, 512), 512), pl.ds(pl.multiple_of(k * 1024, 1024), 1024), 8)
        for i in range(1, 5):
            @pl.when(b == i)
            def _():
                finish(LARGE[i][0])
        return carry

    lax.fori_loop(0, len(SMALL), small, 0)
    lax.fori_loop(0, len(LARGE), large, 0)

    for h in (0, 1):
        for d in range(1, 8):
            ring(d, h).wait_send()
        for d in range(8):
            across(d, h).wait_send()
        for i in (1, 2, 3):
            query1(h, i).wait_send()
            query2(h, i, 0).wait_send()
            query2(h, i, 1).wait_send()

    for p, h in ((0, 0), (0, 1), (1, 0), (1, 1)):
        for i in (2, 1, 3):
            for c in result1(h, i, p):
                c.wait_recv()
        stats = [stat[2 * h + p]] + [stat1[h, j, p] for j in range(3)]
        m, l, sl = ([s[r:r + 1, :] for s in stats] for r in range(3))
        top = jnp.maximum(jnp.maximum(m[0], m[1]), jnp.maximum(m[2], m[3]))
        wgt = [jnp.exp2(a - top) * b for a, b in zip(m, l)]
        total = wgt[0] + wgt[1] + wgt[2] + wgt[3]
        inv = 1.0 / total
        wgt = [a * inv for a in wgt]
        mean = wgt[0] * sl[0] + wgt[1] * sl[1] + wgt[2] * sl[2] + wgt[3] * sl[3]
        sstat1[h, p, 0:1, :] = top
        sstat1[h, p, 1:2, :] = total
        sstat1[h, p, 2:3, :] = mean
        sstat1[h, p, 3:8, :] = jnp.zeros((5, TOK), F32)
        col = jnp.concatenate(wgt + [a * (b - mean) for a, b in zip(wgt, sl)], axis=0).T
        att = jnp.zeros((TOK, HD), F32)
        tan = jnp.zeros((TOK, HD), F32)
        for n in range(4):
            src = part[2 * h + p] if n == 0 else part1[h, n - 1, p]
            a, t = src[:, :128].astype(F32), src[:, 128:].astype(F32)
            att = att + col[:, n:n + 1] * a
            tan = tan + col[:, n:n + 1] * t + col[:, 4 + n:5 + n] * a
        sum1[h, p, :, :128] = att.astype(BF16)
        sum1[h, p, :, 128:] = tan.astype(BF16)
        for i in ((1,), (2, 3))[p]:
            for c in result2(h, i):
                c.start()

    for h in (0, 1):
        for i in (1, 2, 3):
            for c in result1(h, i, 0) + result1(h, i, 1):
                c.wait_send()

    for h in (0, 1):
        for i in (1, 3, 2):
            for c in result2(h, i):
                c.wait_recv()
        cols = [sstat1[h, 0].T[0:HALF, :]]
        srcs = [sum1[h, 0, 0:HALF, :]]
        for b in (1, 2, 3):
            at = (4 - b) % 2 * HALF
            cols.append(stat2[h, b - 1].T[at:at + HALF, :])
            srcs.append(part2[h, b - 1])
        m, l, sl = ([c[:, r:r + 1] for c in cols] for r in range(3))
        top = jnp.maximum(jnp.maximum(m[0], m[1]), jnp.maximum(m[2], m[3]))
        wgt = [jnp.exp2(a - top) * b for a, b in zip(m, l)]
        inv = 1.0 / (wgt[0] + wgt[1] + wgt[2] + wgt[3])
        wgt = [a * inv for a in wgt]
        mean = wgt[0] * sl[0] + wgt[1] * sl[1] + wgt[2] * sl[2] + wgt[3] * sl[3]
        att = jnp.zeros((HALF, HD), F32)
        tan = jnp.zeros((HALF, HD), F32)
        for n in range(4):
            a, t = srcs[n][:, :128].astype(F32), srcs[n][:, 128:].astype(F32)
            att = att + wgt[n] * a
            tan = tan + wgt[n] * t + (wgt[n] * (sl[n] - mean)) * a
        out_ref[h * HALF:(h + 1) * HALF, :] = att
        out_ref[TOK + h * HALF:TOK + (h + 1) * HALF, :] = tan

    for h in (0, 1):
        for i in (1, 2, 3):
            for c in result2(h, i):
                c.wait_send()


def on_device(query_rows, key_rows, value_rows, query_tangent, key_tangent, value_tangent):
    dma = pltpu.SemaphoreType.DMA
    both = pl.pallas_call(
        kernel,
        out_shape=jax.ShapeDtypeStruct((2 * TOK, HD), F32),
        in_specs=[pl.BlockSpec(memory_space=pl.ANY)] * 6,
        out_specs=pl.BlockSpec(memory_space=pltpu.VMEM),
        scratch_shapes=[
            pltpu.VMEM((NK, 512), BF16),
            pltpu.VMEM((NQ, 256), BF16),
            pltpu.VMEM((NQ, 384), F32),
            pltpu.VMEM((NQ, 128), F32),
            pltpu.VMEM((NQ, 128), F32),
            pltpu.VMEM((NQ, 128), F32),
            pltpu.VMEM((16, TOK, 256), BF16),
            pltpu.VMEM((16, 8, TOK), F32),
            pltpu.VMEM((2, 3, 2, TOK, 256), BF16),
            pltpu.VMEM((2, 3, 2, 8, TOK), F32),
            pltpu.VMEM((2, 2, TOK, 256), BF16),
            pltpu.VMEM((2, 2, 8, TOK), F32),
            pltpu.VMEM((2, 3, HALF, 256), BF16),
            pltpu.VMEM((2, 3, 8, TOK), F32),
            dma((8,)), dma((8, 2)), dma((8, 2)), dma((8, 2)), dma((8, 2)),
            dma((2, 4)), dma((2, 4)), dma((2, 8)), dma((2, 8)),
            dma((2, 8)), dma((2, 8)), dma((2, 8)), dma((2, 8)),
            dma((2, 4)), dma((2, 4)), dma((2, 4)), dma((2, 4)),
        ],
        compiler_params=pltpu.CompilerParams(
            collective_id=0, has_side_effects=True, vmem_limit_bytes=32 << 20),
    )(*[pltpu.with_memory_space_constraint(a, pltpu.HBM) for a in (query_rows, key_rows, value_rows, query_tangent, key_tangent, value_tangent)])
    return both[:TOK], both[TOK:]


def solution(mesh):
    placed = P(("blk", "grp"), None)
    return jax.shard_map(
        on_device,
        mesh=mesh,
        in_specs=(placed,) * 6,
        out_specs=(placed, placed),
        check_vma=False,
    )
```

```python
import jax
import jax.numpy as jnp
from jax import lax
from jax.experimental import pallas as pl
from jax.experimental.pallas import tpu as pltpu
from jax.sharding import PartitionSpec as P

HD = 128
TOK = 128
HALF = 64
F32, BF16 = jnp.float32, jnp.bfloat16
SCALE = HD ** -0.5
LOG2E = 1.4426950408889634
MESH = pl.DeviceIdType.MESH
NT = (((1,), (1,)), ((), ()))
NQ = 16 * TOK
NK = 16 * TOK

UNIT = ({1: (4, 8), 3: (5, 9), 2: (12, 13)}, {1: (6, 10), 3: (7, 11), 2: (14, 15)})
SENT = {UNIT[h][i][p]: (h, i, p) for h in (0, 1) for i in (1, 2, 3) for p in (0, 1)}
SMALL = [(0, 0), (1, 0), (2, 0), (0, 1), (1, 1), (2, 1)]
LARGE = [(3, 0), (3, 1), (1, 1), (2, 1), (0, 1)]


def pick(i, table):
    out = table[0]
    for n, v in enumerate(table):
        if n > 0:
            out = jnp.where(i == n, v, out)
    return out


def kernel(q_ref, k_ref, v_ref, qt_ref, kt_ref, vt_ref, out_ref,
           kb, qb, acc, mb, lb, wb, part, stat, part1, stat1, sum1, sstat1, part2, stat2,
           in_s, ring_s, ring_r, side_s, side_r, q1_s, q1_r, q2_s, q2_r, o1_s, o1_r, t1_s, t1_r, o2_s, o2_r, t2_s, t2_r):
    blk, grp = lax.axis_index("blk"), lax.axis_index("grp")
    z, x = blk // 8, lax.rem(blk // 2, 4)
    y, core = lax.rem(blk, 2) * 2 + grp // 2, lax.rem(grp, 2)

    def dev(dz=0, dx=0, dy=0, dc=0):
        zz, xx, yy = lax.rem(z + dz, 8), lax.rem(x + dx, 4), lax.rem(y + dy, 4)
        return ((zz * 4 + xx) * 2 + yy // 2, lax.rem(yy, 2) * 2 + lax.rem(core + dc, 2))

    right, left, partner = dev(dz=1), dev(dz=7), dev(dc=1)
    xs, ys = {i: dev(dx=i) for i in (1, 2, 3)}, {i: dev(dy=i) for i in (1, 2, 3)}

    barrier = pltpu.get_barrier_semaphore()
    for d in [right, left, partner] + list(xs.values()) + list(ys.values()):
        pl.semaphore_signal(barrier, inc=1, device_id=d, device_id_type=MESH)

    loads = [pltpu.make_async_copy(src, kb.at[pl.ds(0, TOK), pl.ds(n * HD, HD)], in_s.at[n])
             for n, src in enumerate((kt_ref, k_ref, v_ref, vt_ref))]
    for h in (0, 1):
        for n, src in enumerate((q_ref, qt_ref)):
            loads.append(pltpu.make_async_copy(src.at[pl.ds(h * HALF, HALF), :],
                                               qb.at[pl.ds(h * 256, HALF), pl.ds(n * HD, HD)], in_s.at[4 + 2 * h + n]))
    for c in loads:
        c.start()
    for c in loads:
        c.wait()
    pl.semaphore_wait(barrier, 9)

    def copy(src, dst, ss, rs, to):
        return pltpu.make_async_remote_copy(src_ref=src, dst_ref=dst, send_sem=ss, recv_sem=rs,
                                            device_id=to, device_id_type=MESH)

    def key_half(d, h, side=0):
        return kb.at[pl.ds(d * 256 + side * TOK + h * HALF, HALF), :]

    def ring(d, h):
        src = 0 if d < 3 else (d - 2 if d < 7 else 5 + h)
        to = (right, left)[h] if d == 7 else (right if d % 2 else left)
        return copy(key_half(src, h), key_half(d, h), ring_s.at[d, h], ring_r.at[d, h], to)

    def across(d, h):
        return copy(key_half(d, h), key_half(d, h, 1), side_s.at[d, h], side_r.at[d, h], partner)

    def query1(h, i):
        b = 4 - i
        return copy(qb.at[pl.ds(h * 256, HALF), :], qb.at[pl.ds(h * 256 + b * HALF, HALF), :],
                    q1_s.at[h, b], q1_r.at[h, b], (xs, ys)[h][i])

    def query2(h, i, p):
        b = 4 - i
        return copy(qb.at[pl.ds(h * 256 + p * TOK, TOK), :], qb.at[pl.ds(UNIT[h][b][p] * TOK, TOK), :],
                    q2_s.at[h, 2 * b + p], q2_r.at[h, 2 * b + p], (ys, xs)[h][i])

    def result1(h, i, p):
        b, u = 4 - i, UNIT[h][i][p]
        to, n = (ys, xs)[h][i], 2 * b + p
        return (copy(part.at[u], part1.at[h, b - 1, p], o1_s.at[h, n], o1_r.at[h, n], to),
                copy(stat.at[u], stat1.at[h, b - 1, p], t1_s.at[h, n], t1_r.at[h, n], to))

    def result2(h, i):
        b, p = 4 - i, i // 2
        to = (xs, ys)[h][i]
        return (copy(sum1.at[h, p, pl.ds(i % 2 * HALF, HALF), :], part2.at[h, b - 1], o2_s.at[h, b], o2_r.at[h, b], to),
                copy(sstat1.at[h, p], stat2.at[h, b - 1], t2_s.at[h, b], t2_r.at[h, b], to))

    for h in (0, 1):
        ring(1, h).start()
        ring(2, h).start()
        if h == 0:
            for i in (1, 3, 2):
                query1(0, i).start()
                query1(1, i).start()
        across(0, h).start()

    mb[...] = jnp.full_like(mb, -1e30)
    lb[...] = jnp.zeros_like(lb)
    wb[...] = jnp.zeros_like(wb)
    acc[...] = jnp.zeros_like(acc)

    def arrive(d, h):
        ring(d, h).wait_recv()
        if d < 5:
            ring(d + 2, h).start()
        elif d == 5 + h:
            ring(7, h).start()
        across(d, h).start()

    def side(*slots):
        for d in slots:
            across(d, 0).wait_recv()
            across(d, 1).wait_recv()

    def small_events(b):
        if b == 0:
            arrive(1, 0)
            arrive(2, 0)
            for i in (1, 3, 2):
                query1(0, i).wait_recv()
                query1(1, i).wait_recv()
            for p, i in ((0, 1), (0, 3), (1, 1), (1, 3), (0, 2), (1, 2)):
                query2(0, i, p).start()
                query2(1, i, p).start()
            arrive(1, 1)
            arrive(2, 1)
            side(0, 1)
        elif b == 1:
            arrive(3, 0)
            arrive(4, 0)
            near(0)
        elif b == 2:
            arrive(3, 1)
            arrive(4, 1)
            near(1)
        elif b == 3:
            arrive(5, 0)
            arrive(6, 0)
            side(2, 3)
        elif b == 4:
            arrive(6, 1)
            arrive(5, 1)

    def near(p):
        for i in (1, 3):
            query2(0, i, p).wait_recv()
            query2(1, i, p).wait_recv()

    def large_events(b):
        if b == 0:
            for p in (0, 1):
                query2(0, 2, p).wait_recv()
                query2(1, 2, p).wait_recv()
            arrive(7, 0)
            arrive(7, 1)
        elif b == 1:
            side(4, 5, 6, 7)

    def finish(g):
        for u in range(4 * g, 4 * g + 4):
            rows = slice(u * TOK, (u + 1) * TOK)
            total = jnp.sum(lb[rows, :], axis=1, keepdims=True)
            inv = 1.0 / total
            slope = jnp.sum(wb[rows, :], axis=1, keepdims=True) * inv * SCALE
            att = acc[rows, :128] * inv
            tan = (acc[rows, 128:256] + SCALE * acc[rows, 256:384]) * inv - slope * att
            part[u, :, :128] = att.astype(BF16)
            part[u, :, 128:] = tan.astype(BF16)
            lane = lax.broadcasted_iota(jnp.int32, (TOK, 128), 1)
            stat[u] = jnp.where(lane == 0, mb[rows, :], jnp.where(lane == 1, total, slope)).T[:8, :]
            if u >= 4:
                for c in result1(*SENT[u]):
                    c.start()

    def attend(first, keys, size):
        cut = [slice(j * 128, (j + 1) * 128) for j in range(size // 128)]
        halves = [pl.ds(pl.multiple_of(first + n * 256, 256), 256) for n in (0, 1)]

        def scores(rows):
            return (lax.dot_general(qb[rows, :128], kb[keys, 128:256], NT, preferred_element_type=F32),
                    lax.dot_general(qb[rows, :], kb[keys, :256], NT, preferred_element_type=F32))

        def soften(rows, s, t):
            top = s[:, cut[0]]
            for j in cut[1:]:
                top = jnp.maximum(top, s[:, j])
            top = jnp.broadcast_to(jnp.max(top, axis=1, keepdims=True), top.shape) * (SCALE * LOG2E)
            old = mb[rows, :]
            new = jnp.maximum(old, top)
            p = [jnp.exp2(s[:, j] * (SCALE * LOG2E) - new) for j in cut]
            w = [a * t[:, j] for a, j in zip(p, cut)]
            return (new, jnp.exp2(old - new), sum(p[1:], p[0]), sum(w[1:], w[0]),
                    jnp.concatenate([a.astype(BF16) for a in p], axis=1),
                    jnp.concatenate([a.astype(BF16) for a in w], axis=1))

        def products(p, w):
            return (jnp.dot(p, kb[keys, 256:512], preferred_element_type=F32),
                    jnp.dot(w, kb[keys, 256:384], preferred_element_type=F32))

        s0 = scores(halves[0])
        s1 = scores(halves[1])
        e0 = soften(halves[0], *s0)
        e1 = soften(halves[1], *s1)
        o0 = products(*e0[4:])
        o1 = products(*e1[4:])
        for rows, (new, al, ps, ws, _, _), (pv, wv) in zip(halves, (e0, e1), (o0, o1)):
            mb[rows, :] = new
            lb[rows, :] = lb[rows, :] * al + ps
            wb[rows, :] = wb[rows, :] * al + ws
            acc[rows, :128] = acc[rows, :128] * al + pv[:, :128]
            acc[rows, 128:256] = acc[rows, 128:256] * al + pv[:, 128:]
            acc[rows, 256:384] = acc[rows, 256:384] * al + wv

    def small(b, carry):
        for i in range(6):
            @pl.when(b == i)
            def _():
                small_events(i)
        g, k = pick(b, [e[0] for e in SMALL]), pick(b, [e[1] for e in SMALL])
        attend(g * 512, pl.ds(pl.multiple_of(k * 512, 512), 512), 512)
        return carry

    def large(b, carry):
        for i in range(2):
            @pl.when(b == i)
            def _():
                large_events(i)
        g, k = pick(b, [e[0] for e in LARGE]), pick(b, [e[1] for e in LARGE])
        attend(g * 512, pl.ds(pl.multiple_of(k * 1024, 1024), 1024), 1024)
        for i in range(1, 5):
            @pl.when(b == i)
            def _():
                finish(LARGE[i][0])
        return carry

    lax.fori_loop(0, len(SMALL), small, 0)
    lax.fori_loop(0, len(LARGE), large, 0)

    for h in (0, 1):
        for d in range(1, 8):
            ring(d, h).wait_send()
        for d in range(8):
            across(d, h).wait_send()
        for i in (1, 2, 3):
            query1(h, i).wait_send()
            query2(h, i, 0).wait_send()
            query2(h, i, 1).wait_send()

    for p, h in ((0, 0), (0, 1), (1, 0), (1, 1)):
        for i in (2, 1, 3):
            for c in result1(h, i, p):
                c.wait_recv()
        stats = [stat[2 * h + p]] + [stat1[h, j, p] for j in range(3)]
        m, l, sl = ([s[r:r + 1, :] for s in stats] for r in range(3))
        top = jnp.maximum(jnp.maximum(m[0], m[1]), jnp.maximum(m[2], m[3]))
        wgt = [jnp.exp2(a - top) * b for a, b in zip(m, l)]
        total = wgt[0] + wgt[1] + wgt[2] + wgt[3]
        inv = 1.0 / total
        wgt = [a * inv for a in wgt]
        mean = wgt[0] * sl[0] + wgt[1] * sl[1] + wgt[2] * sl[2] + wgt[3] * sl[3]
        sstat1[h, p, 0:1, :] = top
        sstat1[h, p, 1:2, :] = total
        sstat1[h, p, 2:3, :] = mean
        sstat1[h, p, 3:8, :] = jnp.zeros((5, TOK), F32)
        col = jnp.concatenate(wgt + [a * (b - mean) for a, b in zip(wgt, sl)], axis=0).T
        att = jnp.zeros((TOK, HD), F32)
        tan = jnp.zeros((TOK, HD), F32)
        for n in range(4):
            src = part[2 * h + p] if n == 0 else part1[h, n - 1, p]
            a, t = src[:, :128].astype(F32), src[:, 128:].astype(F32)
            att = att + col[:, n:n + 1] * a
            tan = tan + col[:, n:n + 1] * t + col[:, 4 + n:5 + n] * a
        sum1[h, p, :, :128] = att.astype(BF16)
        sum1[h, p, :, 128:] = tan.astype(BF16)
        for i in ((1,), (2, 3))[p]:
            for c in result2(h, i):
                c.start()

    for h in (0, 1):
        for i in (1, 2, 3):
            for c in result1(h, i, 0) + result1(h, i, 1):
                c.wait_send()

    for h in (0, 1):
        for i in (1, 3, 2):
            for c in result2(h, i):
                c.wait_recv()
        cols = [sstat1[h, 0].T[0:HALF, :]]
        srcs = [sum1[h, 0, 0:HALF, :]]
        for b in (1, 2, 3):
            at = (4 - b) % 2 * HALF
            cols.append(stat2[h, b - 1].T[at:at + HALF, :])
            srcs.append(part2[h, b - 1])
        m, l, sl = ([c[:, r:r + 1] for c in cols] for r in range(3))
        top = jnp.maximum(jnp.maximum(m[0], m[1]), jnp.maximum(m[2], m[3]))
        wgt = [jnp.exp2(a - top) * b for a, b in zip(m, l)]
        inv = 1.0 / (wgt[0] + wgt[1] + wgt[2] + wgt[3])
        wgt = [a * inv for a in wgt]
        mean = wgt[0] * sl[0] + wgt[1] * sl[1] + wgt[2] * sl[2] + wgt[3] * sl[3]
        att = jnp.zeros((HALF, HD), F32)
        tan = jnp.zeros((HALF, HD), F32)
        for n in range(4):
            a, t = srcs[n][:, :128].astype(F32), srcs[n][:, 128:].astype(F32)
            att = att + wgt[n] * a
            tan = tan + wgt[n] * t + (wgt[n] * (sl[n] - mean)) * a
        out_ref[h * HALF:(h + 1) * HALF, :] = att
        out_ref[TOK + h * HALF:TOK + (h + 1) * HALF, :] = tan

    for h in (0, 1):
        for i in (1, 2, 3):
            for c in result2(h, i):
                c.wait_send()


def on_device(query_rows, key_rows, value_rows, query_tangent, key_tangent, value_tangent):
    dma = pltpu.SemaphoreType.DMA
    both = pl.pallas_call(
        kernel,
        out_shape=jax.ShapeDtypeStruct((2 * TOK, HD), F32),
        in_specs=[pl.BlockSpec(memory_space=pl.ANY)] * 6,
        out_specs=pl.BlockSpec(memory_space=pltpu.VMEM),
        scratch_shapes=[
            pltpu.VMEM((NK, 512), BF16),
            pltpu.VMEM((NQ, 256), BF16),
            pltpu.VMEM((NQ, 384), F32),
            pltpu.VMEM((NQ, 128), F32),
            pltpu.VMEM((NQ, 128), F32),
            pltpu.VMEM((NQ, 128), F32),
            pltpu.VMEM((16, TOK, 256), BF16),
            pltpu.VMEM((16, 8, TOK), F32),
            pltpu.VMEM((2, 3, 2, TOK, 256), BF16),
            pltpu.VMEM((2, 3, 2, 8, TOK), F32),
            pltpu.VMEM((2, 2, TOK, 256), BF16),
            pltpu.VMEM((2, 2, 8, TOK), F32),
            pltpu.VMEM((2, 3, HALF, 256), BF16),
            pltpu.VMEM((2, 3, 8, TOK), F32),
            dma((8,)), dma((8, 2)), dma((8, 2)), dma((8, 2)), dma((8, 2)),
            dma((2, 4)), dma((2, 4)), dma((2, 8)), dma((2, 8)),
            dma((2, 8)), dma((2, 8)), dma((2, 8)), dma((2, 8)),
            dma((2, 4)), dma((2, 4)), dma((2, 4)), dma((2, 4)),
        ],
        compiler_params=pltpu.CompilerParams(
            collective_id=0, has_side_effects=True, vmem_limit_bytes=32 << 20),
    )(*[pltpu.with_memory_space_constraint(a, pltpu.HBM) for a in (query_rows, key_rows, value_rows, query_tangent, key_tangent, value_tangent)])
    return both[:TOK], both[TOK:]


def solution(mesh):
    placed = P(("blk", "grp"), None)
    return jax.shard_map(
        on_device,
        mesh=mesh,
        in_specs=(placed,) * 6,
        out_specs=(placed, placed),
        check_vma=False,
    )
```

```python
import jax
import jax.numpy as jnp
from jax import lax
from jax.experimental import pallas as pl
from jax.experimental.pallas import tpu as pltpu
from jax.sharding import PartitionSpec as P

HD = 128
TOK = 128
HALF = 64
F32, BF16 = jnp.float32, jnp.bfloat16
SCALE = HD ** -0.5
LOG2E = 1.4426950408889634
MESH = pl.DeviceIdType.MESH
NT = (((1,), (1,)), ((), ()))
NQ = 16 * TOK
NK = 16 * TOK

UNIT = ({1: (4, 8), 3: (5, 9), 2: (12, 13)}, {1: (6, 10), 3: (7, 11), 2: (14, 15)})
SENT = {UNIT[h][i][p]: (h, i, p) for h in (0, 1) for i in (1, 2, 3) for p in (0, 1)}
SMALL = [(0, 0), (1, 0), (2, 0), (0, 1), (1, 1), (2, 1)]
LARGE = [(3, 0), (3, 1), (1, 1), (2, 1), (0, 1)]


def pick(i, table):
    out = table[0]
    for n, v in enumerate(table):
        if n > 0:
            out = jnp.where(i == n, v, out)
    return out


def kernel(q_ref, k_ref, v_ref, qt_ref, kt_ref, vt_ref, out_ref,
           kb, qb, acc, mb, lb, wb, part, stat, part1, stat1, sum1, sstat1, part2, stat2,
           in_s, ring_s, ring_r, side_s, side_r, q1_s, q1_r, q2_s, q2_r, o1_s, o1_r, t1_s, t1_r, o2_s, o2_r, t2_s, t2_r):
    blk, grp = lax.axis_index("blk"), lax.axis_index("grp")
    z, x = blk // 8, lax.rem(blk // 2, 4)
    y, core = lax.rem(blk, 2) * 2 + grp // 2, lax.rem(grp, 2)

    def dev(dz=0, dx=0, dy=0, dc=0):
        zz, xx, yy = lax.rem(z + dz, 8), lax.rem(x + dx, 4), lax.rem(y + dy, 4)
        return ((zz * 4 + xx) * 2 + yy // 2, lax.rem(yy, 2) * 2 + lax.rem(core + dc, 2))

    right, left, partner = dev(dz=1), dev(dz=7), dev(dc=1)
    xs, ys = {i: dev(dx=i) for i in (1, 2, 3)}, {i: dev(dy=i) for i in (1, 2, 3)}

    barrier = pltpu.get_barrier_semaphore()
    for d in [right, left, partner] + list(xs.values()) + list(ys.values()):
        pl.semaphore_signal(barrier, inc=1, device_id=d, device_id_type=MESH)

    loads = [pltpu.make_async_copy(src, kb.at[pl.ds(0, TOK), pl.ds(n * HD, HD)], in_s.at[n])
             for n, src in enumerate((kt_ref, k_ref, v_ref, vt_ref))]
    for h in (0, 1):
        for n, src in enumerate((q_ref, qt_ref)):
            loads.append(pltpu.make_async_copy(src.at[pl.ds(h * HALF, HALF), :],
                                               qb.at[pl.ds(h * 256, HALF), pl.ds(n * HD, HD)], in_s.at[4 + 2 * h + n]))
    for c in loads:
        c.start()
    for c in loads[:4]:
        c.wait()
    pl.semaphore_wait(barrier, 9)

    def copy(src, dst, ss, rs, to):
        return pltpu.make_async_remote_copy(src_ref=src, dst_ref=dst, send_sem=ss, recv_sem=rs,
                                            device_id=to, device_id_type=MESH)

    def key_half(d, h, side=0):
        return kb.at[pl.ds(d * 256 + side * TOK + h * HALF, HALF), :]

    def ring(d, h):
        src = 0 if d < 3 else (d - 2 if d < 7 else 5 + h)
        to = (right, left)[h] if d == 7 else (right if d % 2 else left)
        return copy(key_half(src, h), key_half(d, h), ring_s.at[d, h], ring_r.at[d, h], to)

    def across(d, h):
        return copy(key_half(d, h), key_half(d, h, 1), side_s.at[d, h], side_r.at[d, h], partner)

    def query1(h, i):
        b = 4 - i
        return copy(qb.at[pl.ds(h * 256, HALF), :], qb.at[pl.ds(h * 256 + b * HALF, HALF), :],
                    q1_s.at[h, b], q1_r.at[h, b], (xs, ys)[h][i])

    def query2(h, i, p):
        b = 4 - i
        return copy(qb.at[pl.ds(h * 256 + p * TOK, TOK), :], qb.at[pl.ds(UNIT[h][b][p] * TOK, TOK), :],
                    q2_s.at[h, 2 * b + p], q2_r.at[h, 2 * b + p], (ys, xs)[h][i])

    def result1(h, i, p):
        b, u = 4 - i, UNIT[h][i][p]
        to, n = (ys, xs)[h][i], 2 * b + p
        return (copy(part.at[u], part1.at[h, b - 1, p], o1_s.at[h, n], o1_r.at[h, n], to),
                copy(stat.at[u], stat1.at[h, b - 1, p], t1_s.at[h, n], t1_r.at[h, n], to))

    def result2(h, i):
        b, p = 4 - i, i // 2
        to = (xs, ys)[h][i]
        return (copy(sum1.at[h, p, pl.ds(i % 2 * HALF, HALF), :], part2.at[h, b - 1], o2_s.at[h, b], o2_r.at[h, b], to),
                copy(sstat1.at[h, p], stat2.at[h, b - 1], t2_s.at[h, b], t2_r.at[h, b], to))

    for h in (0, 1):
        ring(1, h).start()
        ring(2, h).start()
        if h == 0:
            for c in loads[4:]:
                c.wait()
            for i in (1, 3, 2):
                query1(0, i).start()
                query1(1, i).start()
        across(0, h).start()

    mb[...] = jnp.full_like(mb, -1e30)
    lb[...] = jnp.zeros_like(lb)
    wb[...] = jnp.zeros_like(wb)
    acc[...] = jnp.zeros_like(acc)

    def arrive(d, h):
        ring(d, h).wait_recv()
        if d < 5:
            ring(d + 2, h).start()
        elif d == 5 + h:
            ring(7, h).start()
        across(d, h).start()

    def side(*slots):
        for d in slots:
            across(d, 0).wait_recv()
            across(d, 1).wait_recv()

    def small_events(b):
        if b == 0:
            arrive(1, 0)
            arrive(2, 0)
            for i in (1, 3, 2):
                query1(0, i).wait_recv()
                query1(1, i).wait_recv()
            for p, i in ((0, 1), (0, 3), (1, 1), (1, 3), (0, 2), (1, 2)):
                query2(0, i, p).start()
                query2(1, i, p).start()
            arrive(1, 1)
            arrive(2, 1)
            side(0, 1)
        elif b == 1:
            arrive(3, 0)
            arrive(4, 0)
            near(0)
        elif b == 2:
            arrive(3, 1)
            arrive(4, 1)
            near(1)
        elif b == 3:
            arrive(5, 0)
            arrive(6, 0)
            side(2, 3)
        elif b == 4:
            arrive(6, 1)
            arrive(5, 1)

    def near(p):
        for i in (1, 3):
            query2(0, i, p).wait_recv()
            query2(1, i, p).wait_recv()

    def large_events(b):
        if b == 0:
            for p in (0, 1):
                query2(0, 2, p).wait_recv()
                query2(1, 2, p).wait_recv()
            arrive(7, 0)
            arrive(7, 1)
        elif b == 1:
            side(4, 5, 6, 7)

    def finish(g):
        for u in range(4 * g, 4 * g + 4):
            rows = slice(u * TOK, (u + 1) * TOK)
            total = jnp.sum(lb[rows, :], axis=1, keepdims=True)
            inv = 1.0 / total
            slope = jnp.sum(wb[rows, :], axis=1, keepdims=True) * inv * SCALE
            att = acc[rows, :128] * inv
            tan = (acc[rows, 128:256] + SCALE * acc[rows, 256:384]) * inv - slope * att
            part[u, :, :128] = att.astype(BF16)
            part[u, :, 128:] = tan.astype(BF16)
            lane = lax.broadcasted_iota(jnp.int32, (TOK, 128), 1)
            stat[u] = jnp.where(lane == 0, mb[rows, :], jnp.where(lane == 1, total, slope)).T[:8, :]
            if u >= 4:
                for c in result1(*SENT[u]):
                    c.start()

    def attend(first, keys, size):
        cut = [slice(j * 128, (j + 1) * 128) for j in range(size // 128)]
        halves = [pl.ds(pl.multiple_of(first + n * 256, 256), 256) for n in (0, 1)]

        def scores(rows):
            return (lax.dot_general(qb[rows, :128], kb[keys, 128:256], NT, preferred_element_type=F32),
                    lax.dot_general(qb[rows, :], kb[keys, :256], NT, preferred_element_type=F32))

        def soften(rows, s, t):
            top = s[:, cut[0]]
            for j in cut[1:]:
                top = jnp.maximum(top, s[:, j])
            top = jnp.broadcast_to(jnp.max(top, axis=1, keepdims=True), top.shape) * (SCALE * LOG2E)
            old = mb[rows, :]
            new = jnp.maximum(old, top)
            p = [jnp.exp2(s[:, j] * (SCALE * LOG2E) - new) for j in cut]
            w = [a * t[:, j] for a, j in zip(p, cut)]
            return (new, jnp.exp2(old - new), sum(p[1:], p[0]), sum(w[1:], w[0]),
                    jnp.concatenate([a.astype(BF16) for a in p], axis=1),
                    jnp.concatenate([a.astype(BF16) for a in w], axis=1))

        def products(p, w):
            return (jnp.dot(p, kb[keys, 256:512], preferred_element_type=F32),
                    jnp.dot(w, kb[keys, 256:384], preferred_element_type=F32))

        s0 = scores(halves[0])
        s1 = scores(halves[1])
        e0 = soften(halves[0], *s0)
        e1 = soften(halves[1], *s1)
        o0 = products(*e0[4:])
        o1 = products(*e1[4:])
        for rows, (new, al, ps, ws, _, _), (pv, wv) in zip(halves, (e0, e1), (o0, o1)):
            mb[rows, :] = new
            lb[rows, :] = lb[rows, :] * al + ps
            wb[rows, :] = wb[rows, :] * al + ws
            acc[rows, :128] = acc[rows, :128] * al + pv[:, :128]
            acc[rows, 128:256] = acc[rows, 128:256] * al + pv[:, 128:]
            acc[rows, 256:384] = acc[rows, 256:384] * al + wv

    def small(b, carry):
        for i in range(6):
            @pl.when(b == i)
            def _():
                small_events(i)
        g, k = pick(b, [e[0] for e in SMALL]), pick(b, [e[1] for e in SMALL])
        attend(g * 512, pl.ds(pl.multiple_of(k * 512, 512), 512), 512)
        return carry

    def large(b, carry):
        for i in range(2):
            @pl.when(b == i)
            def _():
                large_events(i)
        g, k = pick(b, [e[0] for e in LARGE]), pick(b, [e[1] for e in LARGE])
        attend(g * 512, pl.ds(pl.multiple_of(k * 1024, 1024), 1024), 1024)
        for i in range(1, 5):
            @pl.when(b == i)
            def _():
                finish(LARGE[i][0])
        return carry

    lax.fori_loop(0, len(SMALL), small, 0)
    lax.fori_loop(0, len(LARGE), large, 0)

    for h in (0, 1):
        for d in range(1, 8):
            ring(d, h).wait_send()
        for d in range(8):
            across(d, h).wait_send()
        for i in (1, 2, 3):
            query1(h, i).wait_send()
            query2(h, i, 0).wait_send()
            query2(h, i, 1).wait_send()

    for p, h in ((0, 0), (0, 1), (1, 0), (1, 1)):
        for i in (2, 1, 3):
            for c in result1(h, i, p):
                c.wait_recv()
        stats = [stat[2 * h + p]] + [stat1[h, j, p] for j in range(3)]
        m, l, sl = ([s[r:r + 1, :] for s in stats] for r in range(3))
        top = jnp.maximum(jnp.maximum(m[0], m[1]), jnp.maximum(m[2], m[3]))
        wgt = [jnp.exp2(a - top) * b for a, b in zip(m, l)]
        total = wgt[0] + wgt[1] + wgt[2] + wgt[3]
        inv = 1.0 / total
        wgt = [a * inv for a in wgt]
        mean = wgt[0] * sl[0] + wgt[1] * sl[1] + wgt[2] * sl[2] + wgt[3] * sl[3]
        sstat1[h, p, 0:1, :] = top
        sstat1[h, p, 1:2, :] = total
        sstat1[h, p, 2:3, :] = mean
        sstat1[h, p, 3:8, :] = jnp.zeros((5, TOK), F32)
        col = jnp.concatenate(wgt + [a * (b - mean) for a, b in zip(wgt, sl)], axis=0).T
        att = jnp.zeros((TOK, HD), F32)
        tan = jnp.zeros((TOK, HD), F32)
        for n in range(4):
            src = part[2 * h + p] if n == 0 else part1[h, n - 1, p]
            a, t = src[:, :128].astype(F32), src[:, 128:].astype(F32)
            att = att + col[:, n:n + 1] * a
            tan = tan + col[:, n:n + 1] * t + col[:, 4 + n:5 + n] * a
        sum1[h, p, :, :128] = att.astype(BF16)
        sum1[h, p, :, 128:] = tan.astype(BF16)
        for i in ((1,), (2, 3))[p]:
            for c in result2(h, i):
                c.start()

    for h in (0, 1):
        for i in (1, 2, 3):
            for c in result1(h, i, 0) + result1(h, i, 1):
                c.wait_send()

    for h in (0, 1):
        for i in (1, 3, 2):
            for c in result2(h, i):
                c.wait_recv()
        cols = [sstat1[h, 0].T[0:HALF, :]]
        srcs = [sum1[h, 0, 0:HALF, :]]
        for b in (1, 2, 3):
            at = (4 - b) % 2 * HALF
            cols.append(stat2[h, b - 1].T[at:at + HALF, :])
            srcs.append(part2[h, b - 1])
        m, l, sl = ([c[:, r:r + 1] for c in cols] for r in range(3))
        top = jnp.maximum(jnp.maximum(m[0], m[1]), jnp.maximum(m[2], m[3]))
        wgt = [jnp.exp2(a - top) * b for a, b in zip(m, l)]
        inv = 1.0 / (wgt[0] + wgt[1] + wgt[2] + wgt[3])
        wgt = [a * inv for a in wgt]
        mean = wgt[0] * sl[0] + wgt[1] * sl[1] + wgt[2] * sl[2] + wgt[3] * sl[3]
        att = jnp.zeros((HALF, HD), F32)
        tan = jnp.zeros((HALF, HD), F32)
        for n in range(4):
            a, t = srcs[n][:, :128].astype(F32), srcs[n][:, 128:].astype(F32)
            att = att + wgt[n] * a
            tan = tan + wgt[n] * t + (wgt[n] * (sl[n] - mean)) * a
        out_ref[h * HALF:(h + 1) * HALF, :] = att
        out_ref[TOK + h * HALF:TOK + (h + 1) * HALF, :] = tan

    for h in (0, 1):
        for i in (1, 2, 3):
            for c in result2(h, i):
                c.wait_send()


def on_device(query_rows, key_rows, value_rows, query_tangent, key_tangent, value_tangent):
    dma = pltpu.SemaphoreType.DMA
    both = pl.pallas_call(
        kernel,
        out_shape=jax.ShapeDtypeStruct((2 * TOK, HD), F32),
        in_specs=[pl.BlockSpec(memory_space=pl.ANY)] * 6,
        out_specs=pl.BlockSpec(memory_space=pltpu.VMEM),
        scratch_shapes=[
            pltpu.VMEM((NK, 512), BF16),
            pltpu.VMEM((NQ, 256), BF16),
            pltpu.VMEM((NQ, 384), F32),
            pltpu.VMEM((NQ, 128), F32),
            pltpu.VMEM((NQ, 128), F32),
            pltpu.VMEM((NQ, 128), F32),
            pltpu.VMEM((16, TOK, 256), BF16),
            pltpu.VMEM((16, 8, TOK), F32),
            pltpu.VMEM((2, 3, 2, TOK, 256), BF16),
            pltpu.VMEM((2, 3, 2, 8, TOK), F32),
            pltpu.VMEM((2, 2, TOK, 256), BF16),
            pltpu.VMEM((2, 2, 8, TOK), F32),
            pltpu.VMEM((2, 3, HALF, 256), BF16),
            pltpu.VMEM((2, 3, 8, TOK), F32),
            dma((8,)), dma((8, 2)), dma((8, 2)), dma((8, 2)), dma((8, 2)),
            dma((2, 4)), dma((2, 4)), dma((2, 8)), dma((2, 8)),
            dma((2, 8)), dma((2, 8)), dma((2, 8)), dma((2, 8)),
            dma((2, 4)), dma((2, 4)), dma((2, 4)), dma((2, 4)),
        ],
        compiler_params=pltpu.CompilerParams(
            collective_id=0, has_side_effects=True, vmem_limit_bytes=32 << 20),
    )(*[pltpu.with_memory_space_constraint(a, pltpu.HBM) for a in (query_rows, key_rows, value_rows, query_tangent, key_tangent, value_tangent)])
    return both[:TOK], both[TOK:]


def solution(mesh):
    placed = P(("blk", "grp"), None)
    return jax.shard_map(
        on_device,
        mesh=mesh,
        in_specs=(placed,) * 6,
        out_specs=(placed, placed),
        check_vma=False,
    )
```
